256 devices in a mesh: seq: 32 (over x, y, core), grp: 8 (over z).
Axes of the slice: x: 4, y: 4, z: 8, core: 2. Of those that a mesh axis runs over, the one named last changes fastest.
Arguments:
- query_rows: bfloat16 [16384, 2048], P('seq', 'grp'), may hold values from -6 to 6
- key_rows: bfloat16 [16384, 2048], P('seq', 'grp'), may hold values from -6 to 6
- value_rows: bfloat16 [16384, 2048], P('seq', 'grp'), may hold values from -6 to 6
- attn_output: bfloat16 [16384, 2048], P('seq', 'grp'), may hold values from -6 to 6
- output_grad: bfloat16 [16384, 2048], P('seq', 'grp'), may hold values from -6 to 6
- row_logsumexp: bfloat16 [16, 16384], P('grp', 'seq'), may hold values from 6 to 7.5
- layer_input: bfloat16 [16384, 4096], P('seq', 'grp'), may hold values from -6 to 6
- galore_proj: bfloat16 [4096, 512], P('grp'), may hold values from -0.09375 to 0.09375
- rand_owner: int32 [256, 3], replicated, may hold values from 0 to 31, all different within a row; in each aligned block of 8 rows (0 to 7, 8 to 15, ...) at most 2 rows name the same one
- rand_local: int32 [256, 3], replicated, may hold values from 0 to 7
- global_block: int32 [2], replicated, may hold values from 0 to 255
Outputs:
- grad_query: bfloat16 [16384, 2048], P('seq', 'grp')
- grad_key: bfloat16 [16384, 2048], P('seq', 'grp')
- grad_value: bfloat16 [16384, 2048], P('seq', 'grp')
- clipped_factors: float32 [3, 512, 2048], P(None, 'seq', 'grp')
The draws below stay inside these ranges and needn't reach their ends.
Inputs may be any that keep to these rules, and one draw needn't show every extreme that they name: `rand_owner`: within a row the 3 holders differ; within the rows of one device (aligned blocks of 8 rows) no holder is named more than 2 times, a bound that some block reaches.
All inputs are finite; a program needn't handle non-finite values.
Results may differ from the reference program's by a relative error of at most 0.0063.
Values may be sent and summed in bfloat16 or wider, within the bound.
A program may use at most 128 MiB of HBM per device.

```python
import math
import jax
import jax.numpy as jnp
import numpy as np
from jax import lax

D = 4096
HEADS = 16
HD = 128
RANK = 512
BLK = 64
RAND = 3
NGLOB = 2
NB_DEV = 8
NBT = 256
TOKENS = 16384
HF = 2048
CAP = 2
N_SEQ = 32


def draw_layer_input(key, part):
    base = jax.random.fold_in(key, 101)
    noise_key, offset_key = jax.random.split(base, 2)
    offset = jnp.clip(0.8 * jax.random.normal(offset_key, (D,), jnp.float32), -2.5, 2.5)
    noise = jnp.clip(jax.random.normal(noise_key, (TOKENS, D), jnp.float32), -3.5, 3.5)
    return jnp.clip(noise + offset[None, :], -6.0, 6.0).astype(jnp.bfloat16)


def draw_output_grad(key, part):
    base = jax.random.fold_in(key, 202)
    noise_key, offset_key = jax.random.split(base, 2)
    offset = jnp.clip(0.015 * jax.random.normal(offset_key, (HF,), jnp.float32), -0.1, 0.1)
    noise = jnp.clip(jax.random.normal(noise_key, (TOKENS, HF), jnp.float32), -5.5, 5.5)
    return jnp.clip(noise + offset[None, :], -6.0, 6.0).astype(jnp.bfloat16)


def plant(values, rng, low, largest):
    dims = values.shape
    place = [jax.random.randint(jax.random.fold_in(rng, axis), (), 0, dims[axis]) for axis in range(len(dims))]
    values = values.at[tuple(place)].set(low)
    longest = dims.index(max(dims))
    place[longest] = (place[longest] + 1) % dims[longest]
    return values.at[tuple(place)].set(largest)


def steps_of(rng, extent, shards, smallest, high):
    level, own = 1.0, jax.random.fold_in(rng, 6)
    for axis_at, blocks in shards:
        draws = jnp.exp(jax.random.uniform(jax.random.fold_in(own, axis_at), (blocks,), jnp.float32, smallest / len(shards), high / len(shards)))
        level = level * jnp.repeat(draws, extent[axis_at] // blocks).reshape([-1 if axis == axis_at else 1 for axis in range(len(extent))])
    return level


def shared_out(own_key, own, number, rows, amount, top, reach, lean):
    ranking = jax.random.permutation(own_key, amount)
    heavy_load, usual = portions_of(amount, rows * top, reach, lean, True), portions_of(amount, rows * top, reach, lean, False)
    places = jnp.arange(amount)

    def named(lengths, rotation):
        used = int((lengths > 0).sum())
        fixed = max(1, used // 4)
        passed = fixed + (places - fixed + rotation * (used - fixed)) % max(1, amount - fixed)
        return jnp.zeros((amount,), jnp.int32).at[ranking[jnp.where(places < fixed, places, passed)]].set(jnp.asarray(lengths, jnp.int32))

    lengths = jnp.where(number % 4 == 0, named(heavy_load, number // 4), named(usual, number - number // 4 - 1))
    mixed = jax.random.permutation(jax.random.fold_in(own, 3), amount)
    giver, taker = mixed[0:amount // 2 * 2:2], mixed[1:amount // 2 * 2:2]
    room = jnp.minimum(lengths[giver] - 1, reach - lengths[taker]) // 2
    room = jnp.where((giver == ranking[0]) | (taker == ranking[0]) | (lengths[taker] == 0), 0, jnp.maximum(room, 0))
    passed = jax.random.randint(jax.random.fold_in(own, 4), (amount // 2,), 0, 1 << 20) % (room + 1)
    lengths = lengths.at[giver].add(-passed).at[taker].add(passed)
    labels = jnp.searchsorted(jnp.cumsum(lengths), jnp.arange(rows * top), side="right").astype(jnp.int32)
    table = labels.reshape(top, rows).T
    table = table[jax.random.permutation(jax.random.fold_in(own, 1), rows)]
    rotation = jax.random.randint(jax.random.fold_in(own, 2), (rows, 1), 0, top)
    return jnp.take_along_axis(table, (jnp.arange(top)[None, :] + rotation) % top, axis=1)


def portions_of(number_of, total, bound, skew, full):
    portions = [(1 << 20) // math.isqrt(grade ** skew) + 1 for grade in range(1, number_of + 1)]
    largest = bound if full else min(bound, max(-(-total // number_of), total * portions[0] // sum(portions)))
    least = 1 if total - largest >= number_of - 1 else 0
    given, spare = [largest] + [least] * (number_of - 1), total - largest - least * (number_of - 1)
    while spare > 0:
        candidates = [i for i in range(1, number_of) if given[i] < largest] or [i for i in range(1, number_of) if given[i] < bound]
        pool, budget = sum([portions[i] for i in candidates]), spare
        for i in candidates:
            extra = min(bound - given[i], max(1, budget * portions[i] // pool), spare)
            given[i] = given[i] + extra
            spare = spare - extra
    return np.array(given)


def bell_draw(stream_key, extent, width, reach, cuts=(), kind=jnp.bfloat16):
    level = steps_of(stream_key, extent, cuts, -0.22, 0.18) if cuts else 1.0
    values = jax.random.normal(stream_key, extent, jnp.float32) * width * level
    return jnp.minimum(jnp.maximum(values, -reach), reach).astype(kind)


def setup_inputs(seed: int = 0) -> dict:
    seeds = jax.random.split(jax.random.key(seed), 12)
    query_rows = bell_draw(seeds[0], (TOKENS, HF), 1.0, 6.0, ((0, 32), (1, 8)))
    key_rows = bell_draw(seeds[1], (TOKENS, HF), 1.0, 6.0, ((0, 32), (1, 8)))
    value_rows = bell_draw(seeds[2], (TOKENS, HF), 1.0, 6.0, ((0, 32), (1, 8)))
    attn_output = bell_draw(seeds[3], (TOKENS, HF), 1.0, 6.0, ((0, 32), (1, 8)))
    output_grad = draw_output_grad(jax.random.fold_in(seeds[11], 71), 0)
    row_logsumexp = jnp.clip(6.0 + 1.5 * jax.random.uniform(seeds[5], (HEADS, TOKENS), jnp.float32) ** steps_of(seeds[5], (HEADS, TOKENS), ((0, 8), (1, 32)), -0.2, 0.2), 6.0, 7.5).astype(jnp.bfloat16)
    layer_input = draw_layer_input(jax.random.fold_in(seeds[11], 71), 0)
    galore_proj = bell_draw(seeds[7], (D, RANK), D ** -0.5, 0.09375, ((0, 8),))
    rand_owner_keys = jax.random.split(jax.random.fold_in(seeds[8], 1), NBT // NB_DEV)
    rand_owner_turns = jax.random.permutation(jax.random.fold_in(seeds[8], 3), NBT // NB_DEV)
    rand_owner = jax.vmap(lambda own, number: shared_out(jax.random.fold_in(seeds[8], 2), own, number, NB_DEV, N_SEQ, RAND, CAP, 2))(rand_owner_keys, rand_owner_turns).reshape((NBT, RAND))
    rand_local = plant(jax.random.randint(seeds[9], (NBT, RAND), 0, NB_DEV), jax.random.fold_in(seeds[9], 1), 0, NB_DEV - 1).astype(jnp.int32)
    global_block = jax.random.randint(seeds[10], (NGLOB,), 0, NBT).astype(jnp.int32)
    return {"query_rows": query_rows, "key_rows": key_rows, "value_rows": value_rows, "attn_output": attn_output, "output_grad": output_grad, "row_logsumexp": row_logsumexp, "layer_input": layer_input, "galore_proj": galore_proj, "rand_owner": rand_owner, "rand_local": rand_local, "global_block": global_block}


def pair_grads(query_blocks, out_grads, lse_rows, delta_rows, key_blocks, value_blocks, usable):
    head_dim = query_blocks.shape[-1]
    inverse_root = 1.0 / math.sqrt(head_dim)
    query_wide = query_blocks.astype(jnp.float32)
    grad_wide = out_grads.astype(jnp.float32)
    key_wide = key_blocks.astype(jnp.float32)
    value_wide = value_blocks.astype(jnp.float32)
    scores = jnp.einsum('mqhd,mjkhd->mhqjk', query_wide, key_wide) * inverse_root
    lse_heads = jnp.transpose(lse_rows, (0, 2, 1))[:, :, :, None, None]
    delta_heads = jnp.transpose(delta_rows, (0, 2, 1))[:, :, :, None, None]
    weights = jnp.exp(scores - lse_heads) * usable[:, None, None, :, None]
    prob_grad = jnp.einsum('mqhd,mjkhd->mhqjk', grad_wide, value_wide)
    score_grad = weights * (prob_grad - delta_heads) * inverse_root
    weights_low = lax.optimization_barrier(weights.astype(jnp.bfloat16)).astype(jnp.float32)
    score_low = lax.optimization_barrier(score_grad.astype(jnp.bfloat16)).astype(jnp.float32)
    value_grad = jnp.einsum('mhqjk,mqhd->mjkhd', weights_low, grad_wide)
    key_grad = jnp.einsum('mhqjk,mqhd->mjkhd', score_low, query_wide)
    query_grad = jnp.einsum('mhqjk,mjkhd->mqhd', score_low, key_wide)
    return (query_grad, key_grad, value_grad)

def reference(query_rows, key_rows, value_rows, attn_output, output_grad, row_logsumexp, layer_input, galore_proj, rand_owner, rand_local, global_block):
    tokens, feature_width = query_rows.shape
    head_count = HEADS
    head_dim = HD
    total_blocks = tokens // BLK

    def blocked(array):
        return array.reshape(total_blocks, BLK, head_count, head_dim)
    query_blk = blocked(query_rows)
    grad_blk = blocked(output_grad)
    key_blk = blocked(key_rows)
    value_blk = blocked(value_rows)
    lse_blk = row_logsumexp.astype(jnp.float32).reshape(head_count, total_blocks, BLK).transpose(1, 2, 0)
    delta_blk = lax.optimization_barrier(jnp.sum(blocked(output_grad).astype(jnp.float32) * blocked(attn_output).astype(jnp.float32), axis=3))
    block_ids = jnp.arange(total_blocks, dtype=jnp.int32)
    rand_block = (rand_owner * NB_DEV + rand_local).astype(jnp.int32)
    window_ids = jnp.stack([jnp.maximum(block_ids - 1, 0), block_ids, jnp.minimum(block_ids + 1, total_blocks - 1)], axis=1)
    global_ids = jnp.broadcast_to(global_block.astype(jnp.int32)[None, :], (total_blocks, NGLOB))
    key_ids = jnp.concatenate([window_ids, rand_block, global_ids], axis=1).astype(jnp.int32)
    ones_part = jnp.ones((total_blocks, 1 + RAND + NGLOB), jnp.float32)
    left_ok = (block_ids >= 1).astype(jnp.float32)[:, None]
    right_ok = (block_ids < total_blocks - 1).astype(jnp.float32)[:, None]
    usable = jnp.concatenate([left_ok, ones_part[:, :1], right_ok, ones_part[:, 1:]], axis=1)
    entries = key_ids.shape[1]
    group_size = NB_DEV
    group_count = total_blocks // group_size

    def grouped(array):
        return array.reshape((group_count, group_size) + array.shape[1:])

    def scan_step(carry, inputs):
        key_acc, value_acc = carry
        query_group, grad_group, lse_group, delta_group, ids_group, usable_group = inputs
        keys_here = key_blk[ids_group]
        values_here = value_blk[ids_group]
        query_grad, key_grad, value_grad = pair_grads(query_group, grad_group, lse_group, delta_group, keys_here, values_here, usable_group)
        flat_ids = ids_group.reshape(-1)
        key_acc = key_acc.at[flat_ids].add(key_grad.reshape(group_size * entries, BLK, head_count, head_dim))
        value_acc = value_acc.at[flat_ids].add(value_grad.reshape(group_size * entries, BLK, head_count, head_dim))
        return ((key_acc, value_acc), query_grad)
    start_acc = jnp.zeros((total_blocks, BLK, head_count, head_dim), jnp.float32)
    inputs_all = (grouped(query_blk), grouped(grad_blk), grouped(lse_blk), grouped(delta_blk), grouped(key_ids), grouped(usable))
    (key_acc, value_acc), query_parts = lax.scan(scan_step, (start_acc, start_acc), inputs_all)
    grad_query = query_parts.reshape(tokens, feature_width).astype(jnp.bfloat16)
    grad_key = key_acc.reshape(tokens, feature_width).astype(jnp.bfloat16)
    grad_value = value_acc.reshape(tokens, feature_width).astype(jnp.bfloat16)
    projected = jnp.dot(layer_input, galore_proj, preferred_element_type=jnp.float32).astype(jnp.bfloat16)
    factors = jnp.stack([jnp.dot(projected.T, gradient, preferred_element_type=jnp.float32) for gradient in (grad_query, grad_key, grad_value)])
    square_sum = jnp.sum(factors * factors)
    clip_limit = 0.5 * math.sqrt(3 * RANK * feature_width)
    clip_scale = jnp.minimum(1.0, clip_limit * lax.rsqrt(square_sum + 1e-06))
    return (grad_query, grad_key, grad_value, factors * clip_scale)
```

```python
import functools
import math

import jax
import jax.numpy as jnp
from jax import lax
from jax.experimental import pallas as pl
from jax.experimental.pallas import tpu as pltpu
from jax.sharding import PartitionSpec as P

BLK = 64
CAP = 2
MESH = pl.DeviceIdType.MESH
F32 = jnp.float32
BF16 = jnp.bfloat16
FAR = 1e30
VMEM = pltpu.VMEM
ANY = pl.ANY


def vspec():
    return pl.BlockSpec(memory_space=pltpu.VMEM)


def aspec():
    return pl.BlockSpec(memory_space=pl.ANY)


def sspec():
    return pl.BlockSpec(memory_space=pltpu.SMEM)


def params(collective=None, side=False):
    return pltpu.CompilerParams(
        collective_id=collective, has_side_effects=side, vmem_limit_bytes=60 * 1024 * 1024
    )


def mm_nt(a, b):
    return lax.dot_general(a, b, (((1,), (1,)), ((), ())), preferred_element_type=F32)


def mm_tn(a, b):
    return lax.dot_general(a, b, (((0,), (0,)), ((), ())), preferred_element_type=F32)


def mm(a, b):
    return lax.dot_general(a, b, (((1,), (0,)), ((), ())), preferred_element_type=F32)


def rows(at, count):
    return pl.ds(pl.multiple_of(at, count), count)


def pack_kernel(
    pack_ref, glob_ref, q_ref, do_ref, k_ref, v_ref, table_ref, x_ref, g_ref, out_ref, stats_ref, gp_ref, pp_ref
):
    shards = out_ref.shape[0]
    lane_rows = lax.broadcasted_iota(jnp.int32, (8, 128), 0)

    def one(peer, carry):
        tiles = []
        for slot in range(CAP):
            row = pack_ref[peer * CAP + slot]
            safe = jnp.maximum(row, 0)
            out_ref[peer, slot, 0] = q_ref[rows(safe * BLK, BLK), :]
            out_ref[peer, slot, 1] = do_ref[rows(safe * BLK, BLK), :]
            tiles.append(jnp.where(row >= 0, table_ref[safe], FAR))
        stats_ref[peer] = jnp.where(lane_rows < 4, tiles[0], tiles[1])
        return carry

    lax.fori_loop(0, shards, one, 0)
    for number in range(2):
        place = glob_ref[number]
        safe = jnp.maximum(place, 0)
        for side, ref in enumerate((k_ref, v_ref)):
            piece = ref[rows(safe * BLK, BLK), :].astype(F32)
            gp_ref[pl.ds(side * 2 * BLK + number * BLK, BLK), :] = jnp.where(place >= 0, piece, 0.0)
    pp_ref[...] = mm(x_ref[...], g_ref[...])


def peers_of(axis):
    size = lax.axis_size(axis)
    me = lax.axis_index(axis)
    return size, me


def greet(axes):
    barrier = pltpu.get_barrier_semaphore()
    total = 0
    for axis in axes:
        size, me = peers_of(axis)

        def hello(k, carry, axis=axis, size=size, me=me):
            pl.semaphore_signal(
                barrier, inc=1, device_id={axis: lax.rem(me + k, size)}, device_id_type=MESH
            )
            return carry

        lax.fori_loop(1, size, hello, 0)
        total += size - 1
    pl.semaphore_wait(barrier, total)


def send(axis, peer, src, dst, send_sem, recv_sem):
    pltpu.make_async_remote_copy(
        src_ref=src,
        dst_ref=dst,
        send_sem=send_sem,
        recv_sem=recv_sem,
        device_id={axis: peer},
        device_id_type=MESH,
    ).start()


def to_all(axis, src_of, dst_of, send_sem, recv_sem):
    size, me = peers_of(axis)

    def step(k, carry):
        peer = lax.rem(me + k, size)
        send(axis, peer, src_of(peer), dst_of(k), send_sem, recv_sem)
        return carry

    lax.fori_loop(1, size, step, 0)


def drain(ref, sem):
    pltpu.make_async_copy(ref, ref, sem).wait()


def first_kernel(
    pack_ref, stats_ref, k_ref, v_ref, gp_ref, pp_ref,
    arrived_ref, stats_out, halo_ref, gkv_ref, proj_ref,
    gbuf, gown, gall, pbuf, pown, pall, sems, own_sem,
):
    shards, me = peers_of("seq")
    groups, mz = peers_of("grp")
    tokens = k_ref.shape[0]
    gr = gown.shape[0]
    pr = pown.shape[0]
    greet(("seq", "grp"))
    to_all("seq", lambda p: gp_ref.at[rows(p * gr, gr)], lambda k: gbuf.at[k - 1], sems.at[0], sems.at[1])
    to_all("grp", lambda p: pp_ref.at[rows(p * pr, pr)], lambda k: pbuf.at[k - 1], sems.at[2], sems.at[3])
    nxt, prv = lax.rem(me + 1, shards), lax.rem(me + shards - 1, shards)
    for side, ref in enumerate((k_ref, v_ref)):
        send("seq", nxt, ref.at[pl.ds(tokens - BLK, BLK)], halo_ref.at[0, side], sems.at[4], sems.at[5])
        send("seq", prv, ref.at[pl.ds(0, BLK)], halo_ref.at[1, side], sems.at[4], sems.at[5])
    to_all("seq", lambda p: stats_ref.at[p], lambda k: stats_out.at[me], sems.at[6], sems.at[7])
    to_all("seq", lambda p: pack_ref.at[p], lambda k: arrived_ref.at[me], sems.at[8], sems.at[9])
    own = pltpu.make_async_copy(pack_ref.at[me], arrived_ref.at[me], own_sem.at[0])
    own.start()
    own2 = pltpu.make_async_copy(stats_ref.at[me], stats_out.at[me], own_sem.at[1])
    own2.start()
    drain(gbuf, sems.at[1])
    total = gp_ref[rows(me * gr, gr), :]
    for k in range(shards - 1):
        total = total + gbuf[k]
    gown[...] = total
    gall[rows(me * gr, gr), :] = total
    drain(pbuf, sems.at[3])
    ptotal = pp_ref[rows(mz * pr, pr), :]
    for k in range(groups - 1):
        ptotal = ptotal + pbuf[k]
    pown[...] = ptotal.astype(BF16)
    pall[rows(mz * pr, pr), :] = ptotal.astype(BF16)
    to_all("seq", lambda p: gown, lambda k: gall.at[rows(me * gr, gr)], sems.at[10], sems.at[11])
    to_all("grp", lambda p: pown, lambda k: pall.at[rows(mz * pr, pr)], sems.at[12], sems.at[13])
    drain(pall.at[pl.ds(0, pr * (groups - 1))], sems.at[13])
    proj_ref[...] = pall[...]
    drain(gall.at[pl.ds(0, gr * (shards - 1))], sems.at[11])
    gkv_ref[...] = gall[...]
    own.wait()
    own2.wait()
    drain(halo_ref, sems.at[5])
    drain(stats_out.at[pl.ds(0, shards - 1)], sems.at[7])
    drain(arrived_ref.at[pl.ds(0, shards - 1)], sems.at[9])
    drain(gp_ref.at[pl.ds(0, gr * (shards - 1))], sems.at[0])
    drain(pp_ref.at[pl.ds(0, pr * (groups - 1))], sems.at[2])
    drain(halo_ref, sems.at[4])
    drain(stats_ref.at[pl.ds(0, shards - 1)], sems.at[6])
    drain(pack_ref.at[pl.ds(0, shards - 1)], sems.at[8])
    drain(gall.at[pl.ds(0, gr * (shards - 1))], sems.at[10])
    drain(pall.at[pl.ds(0, pr * (groups - 1))], sems.at[12])


def two_heads(block):
    half = block.shape[1] // 2
    lanes = lax.broadcasted_iota(jnp.int32, block.shape, 1)
    zero = jnp.zeros_like(block)
    return jnp.concatenate(
        [jnp.where(lanes < half, block, zero), jnp.where(lanes >= half, block, zero)], axis=0
    )


def pair(q, do, lse, delta, keys, values, good):
    inverse_root = 1.0 / math.sqrt(q.shape[1] // 2)
    qq, dd = two_heads(q), two_heads(do)
    weights = jnp.exp(mm_nt(keys, qq) * inverse_root - lse)
    if good is not None:
        weights = jnp.where(good, weights, 0.0)
    score = weights * (mm_nt(values, dd) - delta) * inverse_root
    weights_low, score_low = weights.astype(BF16), score.astype(BF16)
    dv = mm(weights_low, dd)
    dk = mm(score_low, qq)
    wide = mm_tn(score_low, keys)
    half = q.shape[1] // 2
    dq = jnp.concatenate([wide[:BLK, :half], wide[BLK:, half:]], axis=1)
    return dq, dk, dv


def attend_kernel(
    serve_ref, meta_ref, q_ref, do_ref, k_ref, v_ref, halo_ref, gkv_ref, table_ref, arr_ref, st_ref,
    ret_ref, dq_ref, acc_ref, gacc_ref, kpad, vpad, gk,
):
    i = pl.program_id(0)
    tokens = k_ref.shape[0]

    @pl.when(i == 0)
    def _():
        for pad, ref, side in ((kpad, k_ref, 0), (vpad, v_ref, 1)):
            pad[pl.ds(0, BLK), :] = halo_ref[0, side]
            pad[pl.ds(BLK, tokens), :] = ref[...]
            pad[pl.ds(BLK + tokens, BLK), :] = halo_ref[1, side]
        gk[...] = gkv_ref[...].astype(BF16)
        acc_ref[...] = jnp.zeros_like(acc_ref)
        gacc_ref[...] = jnp.zeros_like(gacc_ref)

    at = i * BLK
    win = pl.ds(pl.multiple_of(at, BLK), 3 * BLK)
    keys = jnp.concatenate([kpad[win, :], gk[: 2 * BLK, :]], axis=0)
    values = jnp.concatenate([vpad[win, :], gk[2 * BLK :, :]], axis=0)
    row = lax.broadcasted_iota(jnp.int32, (5 * BLK, 2 * BLK), 0)
    low = jnp.where(meta_ref[0] == i, BLK, 0)
    high = jnp.where(meta_ref[1] == i, 2 * BLK, 3 * BLK)
    good = ((row >= low) & (row < high)) | (row >= 3 * BLK)
    stat = table_ref[i]
    dq, dk, dv = pair(
        q_ref[rows(at, BLK), :], do_ref[rows(at, BLK), :], stat[0:1, :], stat[1:2, :], keys, values, good
    )
    dq_ref[...] = dq
    acc_ref[0, win, :] += dk[: 3 * BLK]
    acc_ref[1, win, :] += dv[: 3 * BLK]
    gacc_ref[pl.ds(0, 2 * BLK), :] += dk[3 * BLK :]
    gacc_ref[pl.ds(2 * BLK, 2 * BLK), :] += dv[3 * BLK :]
    per = arr_ref.shape[0]
    for p in range(per):
        for c in range(CAP):
            place = serve_ref[(i * per + p) * CAP + c]
            here = rows((place + 1) * BLK, BLK)
            dq, dk, dv = pair(
                arr_ref[p, c, 0], arr_ref[p, c, 1],
                st_ref[p, 4 * c : 4 * c + 1, :], st_ref[p, 4 * c + 1 : 4 * c + 2, :],
                kpad[here, :], vpad[here, :], None,
            )
            ret_ref[p, c] = dq.astype(BF16)
            acc_ref[0, here, :] += dk
            acc_ref[1, here, :] += dv


def second_kernel(
    ret_ref, acc_ref, gacc_ref, back_ref, hg_ref, gsum_ref, gbuf, gown, gall, sems, own_sem
):
    shards, me = peers_of("seq")
    padded = acc_ref.shape[1]
    gr = gown.shape[0]
    greet(("seq",))
    to_all("seq", lambda p: gacc_ref.at[rows(p * gr, gr)], lambda k: gbuf.at[k - 1], sems.at[0], sems.at[1])
    nxt, prv = lax.rem(me + 1, shards), lax.rem(me + shards - 1, shards)
    for side in range(2):
        send("seq", nxt, acc_ref.at[side, pl.ds(padded - BLK, BLK)], hg_ref.at[0, side], sems.at[2], sems.at[3])
        send("seq", prv, acc_ref.at[side, pl.ds(0, BLK)], hg_ref.at[1, side], sems.at[2], sems.at[3])
    to_all("seq", lambda p: ret_ref.at[p], lambda k: back_ref.at[me], sems.at[4], sems.at[5])
    own = pltpu.make_async_copy(ret_ref.at[me], back_ref.at[me], own_sem)
    own.start()
    drain(gbuf, sems.at[1])
    total = gacc_ref[rows(me * gr, gr), :]
    for k in range(shards - 1):
        total = total + gbuf[k]
    gown[...] = total
    gall[rows(me * gr, gr), :] = total
    to_all("seq", lambda p: gown, lambda k: gall.at[rows(me * gr, gr)], sems.at[6], sems.at[7])
    drain(gall.at[pl.ds(0, gr * (shards - 1))], sems.at[7])
    gsum_ref[...] = gall[...]
    own.wait()
    drain(hg_ref, sems.at[3])
    drain(back_ref.at[pl.ds(0, shards - 1)], sems.at[5])
    drain(gbuf, sems.at[0])
    drain(hg_ref, sems.at[2])
    drain(ret_ref.at[pl.ds(0, shards - 1)], sems.at[4])
    drain(gall.at[pl.ds(0, gr * (shards - 1))], sems.at[6])


def finish_kernel(
    fetch_ref, glob_ref, acc_ref, dq_ref, back_ref, hg_ref, gsum_ref, proj_ref,
    gq_ref, gk_ref, gv_ref, part_ref,
):
    blocks = dq_ref.shape[0] // BLK
    randoms = fetch_ref.shape[0] // blocks
    shards = part_ref.shape[0]
    for b in range(blocks):
        here = pl.ds(b * BLK, BLK)
        total = dq_ref[here, :]
        for j in range(randoms):
            slot = fetch_ref[b * randoms + j]
            total = total + back_ref[slot].astype(F32)
        gq_ref[here, :] = total.astype(BF16)
        for side, out in enumerate((gk_ref, gv_ref)):
            total = acc_ref[side, pl.ds((b + 1) * BLK, BLK), :]
            if b == 0:
                total = total + hg_ref[0, side]
            if b == blocks - 1:
                total = total + hg_ref[1, side]
            for number in range(2):
                piece = gsum_ref[pl.ds(side * 2 * BLK + number * BLK, BLK), :]
                total = total + jnp.where(glob_ref[number] == b, piece, 0.0)
            out[here, :] = total.astype(BF16)
    turned = proj_ref[...].astype(F32).T.astype(BF16)
    width = gq_ref.shape[1]
    for number, ref in enumerate((gq_ref, gk_ref, gv_ref)):
        product = mm(turned, ref[...]).astype(BF16)
        share = product.shape[0] // shards
        part_ref[:, pl.ds(number * share, share), :] = product.reshape(shards, share, width)


def clip_kernel(limit, part_ref, out_ref, fbuf, sq, sbuf, sq2, zbuf, sems):
    shards, me = peers_of("seq")
    groups, mz = peers_of("grp")
    greet(("seq", "grp"))
    to_all("seq", lambda p: part_ref.at[p], lambda k: fbuf.at[k - 1], sems.at[0], sems.at[1])
    drain(fbuf, sems.at[1])
    share = part_ref[me].astype(F32)
    for k in range(shards - 1):
        share = share + fbuf[k].astype(F32)
    own = jnp.sum(share * share, keepdims=True)
    tile = jnp.broadcast_to(own, sq.shape)
    sq[...] = tile
    to_all("seq", lambda p: sq, lambda k: sbuf.at[k - 1], sems.at[2], sems.at[3])
    drain(sbuf, sems.at[3])
    for k in range(shards - 1):
        tile = tile + sbuf[k]
    sq2[...] = tile
    to_all("grp", lambda p: sq2, lambda k: zbuf.at[k - 1], sems.at[4], sems.at[5])
    drain(zbuf, sems.at[5])
    for k in range(groups - 1):
        tile = tile + zbuf[k]
    scale = jnp.minimum(1.0, limit * lax.rsqrt(tile[0:1, 0:1] + 1e-06))
    out_ref[...] = share * scale
    drain(fbuf, sems.at[0])
    drain(sbuf, sems.at[2])
    drain(zbuf, sems.at[4])


def slots(match, payload):
    count = match.shape[-1]
    earlier = (jnp.arange(count)[None, :] < jnp.arange(count)[:, None]).astype(jnp.int32)
    rank = jnp.sum(match[..., None, :] * earlier, axis=-1)
    chosen = match[..., None, :] * (rank[..., None, :] == jnp.arange(CAP)[:, None]).astype(jnp.int32)
    live = jnp.sum(chosen, axis=-1)
    value = jnp.sum(chosen * payload[..., None, :], axis=-1)
    return value, live


def body(
    query_rows, key_rows, value_rows, attn_output, output_grad, row_logsumexp,
    layer_input, galore_proj, rand_owner, rand_local, global_block,
):
    tokens, width = query_rows.shape
    heads = row_logsumexp.shape[0]
    blocks = tokens // BLK
    shards, me = peers_of("seq")
    groups = lax.axis_size("grp")
    randoms = rand_owner.shape[1]
    rank = galore_proj.shape[1]
    asks = blocks * randoms
    all_owner = rand_owner.reshape(shards, asks)
    all_local = rand_local.reshape(shards, asks)
    my_owner = lax.dynamic_slice_in_dim(rand_owner, me * blocks, blocks, 0).reshape(asks)
    ask_match = (my_owner[None, :] == jnp.arange(shards, dtype=jnp.int32)[:, None]).astype(jnp.int32)
    row_of = jnp.broadcast_to((jnp.arange(asks, dtype=jnp.int32) // randoms)[None, :], (shards, asks))
    pack_value, pack_live = slots(ask_match, row_of)
    pack_row = jnp.where(pack_live > 0, pack_value, -1).reshape(-1)
    serve_match = (all_owner == me).astype(jnp.int32)
    serve_block = slots(serve_match, all_local)[0].reshape(-1)
    same = (my_owner[:, None] == my_owner[None, :]).astype(jnp.int32)
    before = (jnp.arange(asks)[None, :] < jnp.arange(asks)[:, None]).astype(jnp.int32)
    fetch = my_owner * CAP + jnp.sum(same * before, axis=1)
    glob_place = jnp.where(global_block // blocks == me, global_block % blocks, -1).astype(jnp.int32)
    edges = jnp.stack(
        [jnp.where(me == 0, 0, -1), jnp.where(me == shards - 1, blocks - 1, -1)]
    ).astype(jnp.int32)
    lse = row_logsumexp.astype(F32).reshape(heads, blocks, BLK).transpose(1, 0, 2).reshape(blocks, heads * BLK)
    delta = jnp.sum(
        (output_grad.astype(F32) * attn_output.astype(F32)).reshape(blocks, BLK, heads, width // heads), axis=3
    )
    delta = delta.transpose(0, 2, 1).reshape(blocks, heads * BLK)
    nil = jnp.zeros_like(lse)
    table = jnp.stack([lse, delta, nil, nil, lse, delta, nil, nil], axis=1)

    pack, stats, glob_piece, proj_piece = pl.pallas_call(
        pack_kernel,
        out_shape=(
            jax.ShapeDtypeStruct((shards, CAP, 2, BLK, width), BF16),
            jax.ShapeDtypeStruct((shards, 8, 128), F32),
            jax.ShapeDtypeStruct((4 * BLK, width), F32),
            jax.ShapeDtypeStruct((tokens, rank), F32),
        ),
        in_specs=[sspec()] * 2 + [vspec()] * 7,
        out_specs=(vspec(),) * 4,
        compiler_params=params(),
        name="pack",
    )(pack_row, glob_place, query_rows, output_grad, key_rows, value_rows, table, layer_input, galore_proj)

    gr = 4 * BLK // shards
    pr = tokens // groups
    arrived, stats_in, halo, glob_kv, projected = pl.pallas_call(
        first_kernel,
        out_shape=(
            jax.ShapeDtypeStruct((shards, CAP, 2, BLK, width), BF16),
            jax.ShapeDtypeStruct((shards, 8, 128), F32),
            jax.ShapeDtypeStruct((2, 2, BLK, width), BF16),
            jax.ShapeDtypeStruct((4 * BLK, width), F32),
            jax.ShapeDtypeStruct((tokens, rank), BF16),
        ),
        in_specs=[aspec(), aspec(), aspec(), aspec(), vspec(), vspec()],
        out_specs=(aspec(), aspec(), aspec(), vspec(), vspec()),
        scratch_shapes=[
            VMEM((shards - 1, gr, width), F32),
            VMEM((gr, width), F32),
            VMEM((4 * BLK, width), F32),
            VMEM((groups - 1, pr, rank), F32),
            VMEM((pr, rank), BF16),
            VMEM((tokens, rank), BF16),
            pltpu.SemaphoreType.DMA((14,)),
            pltpu.SemaphoreType.DMA((2,)),
        ],
        compiler_params=params(1, True),
        name="first_exchange",
    )(pack, stats, key_rows, value_rows, glob_piece, proj_piece)

    per = shards // blocks
    full = lambda *shape: pl.BlockSpec(shape, lambda i, *_: (0,) * len(shape))
    back_out, dq_own, acc, gacc = pl.pallas_call(
        attend_kernel,
        grid_spec=pltpu.PrefetchScalarGridSpec(
            num_scalar_prefetch=2,
            grid=(blocks,),
            in_specs=[
                full(tokens, width),
                full(tokens, width),
                full(tokens, width),
                full(tokens, width),
                full(2, 2, BLK, width),
                full(4 * BLK, width),
                full(blocks, 8, 128),
                pl.BlockSpec((per, CAP, 2, BLK, width), lambda i, *_: (i, 0, 0, 0, 0)),
                pl.BlockSpec((per, 8, 128), lambda i, *_: (i, 0, 0)),
            ],
            out_specs=(
                pl.BlockSpec((per, CAP, BLK, width), lambda i, *_: (i, 0, 0, 0)),
                pl.BlockSpec((BLK, width), lambda i, *_: (i, 0)),
                full(2, tokens + 2 * BLK, width),
                full(4 * BLK, width),
            ),
            scratch_shapes=[
                VMEM((tokens + 2 * BLK, width), BF16),
                VMEM((tokens + 2 * BLK, width), BF16),
                VMEM((4 * BLK, width), BF16),
            ],
        ),
        out_shape=(
            jax.ShapeDtypeStruct((shards, CAP, BLK, width), BF16),
            jax.ShapeDtypeStruct((tokens, width), F32),
            jax.ShapeDtypeStruct((2, tokens + 2 * BLK, width), F32),
            jax.ShapeDtypeStruct((4 * BLK, width), F32),
        ),
        compiler_params=params(),
        name="attend",
    )(
        serve_block, edges, query_rows, output_grad, key_rows, value_rows, halo, glob_kv, table, arrived, stats_in
    )

    back, halo_grad, glob_grad = pl.pallas_call(
        second_kernel,
        out_shape=(
            jax.ShapeDtypeStruct((shards, CAP, BLK, width), BF16),
            jax.ShapeDtypeStruct((2, 2, BLK, width), F32),
            jax.ShapeDtypeStruct((4 * BLK, width), F32),
        ),
        in_specs=[aspec(), aspec(), vspec()],
        out_specs=(aspec(), aspec(), vspec()),
        scratch_shapes=[
            VMEM((shards - 1, gr, width), F32),
            VMEM((gr, width), F32),
            VMEM((4 * BLK, width), F32),
            pltpu.SemaphoreType.DMA((8,)),
            pltpu.SemaphoreType.DMA,
        ],
        compiler_params=params(2, True),
        name="second_exchange",
    )(back_out, acc, gacc)

    share = rank // shards
    grad_query, grad_key, grad_value, part = pl.pallas_call(
        finish_kernel,
        out_shape=(
            jax.ShapeDtypeStruct((tokens, width), BF16),
            jax.ShapeDtypeStruct((tokens, width), BF16),
            jax.ShapeDtypeStruct((tokens, width), BF16),
            jax.ShapeDtypeStruct((shards, 3 * share, width), BF16),
        ),
        in_specs=[sspec()] * 2 + [vspec()] * 6,
        out_specs=(vspec(),) * 4,
        compiler_params=params(),
        name="finish",
    )(fetch, glob_place, acc, dq_own, back.reshape(shards * CAP, BLK, width), halo_grad, glob_grad, projected)

    limit = 0.5 * math.sqrt(3 * rank * width * groups)
    clipped = pl.pallas_call(
        functools.partial(clip_kernel, limit),
        out_shape=jax.ShapeDtypeStruct((3 * share, width), F32),
        in_specs=[vspec()],
        out_specs=vspec(),
        scratch_shapes=[
            VMEM((shards - 1, 3 * share, width), BF16),
            VMEM((8, 128), F32),
            VMEM((shards - 1, 8, 128), F32),
            VMEM((8, 128), F32),
            VMEM((groups - 1, 8, 128), F32),
            pltpu.SemaphoreType.DMA((6,)),
        ],
        compiler_params=params(3, True),
        name="clip",
    )(part)
    return (grad_query, grad_key, grad_value, clipped.reshape(3, share, width))


def solution(mesh):
    in_specs = (
        P("seq", "grp"),
        P("seq", "grp"),
        P("seq", "grp"),
        P("seq", "grp"),
        P("seq", "grp"),
        P("grp", "seq"),
        P("seq", "grp"),
        P("grp", None),
        P(),
        P(),
        P(),
    )
    out_specs = (P("seq", "grp"), P("seq", "grp"), P("seq", "grp"), P(None, "seq", "grp"))
    return jax.shard_map(body, mesh=mesh, in_specs=in_specs, out_specs=out_specs, check_vma=False)
```

```python
import functools
import math

import jax
import jax.numpy as jnp
from jax import lax
from jax.experimental import pallas as pl
from jax.experimental.pallas import tpu as pltpu
from jax.sharding import PartitionSpec as P

BLK = 64
CAP = 2
MESH = pl.DeviceIdType.MESH
F32 = jnp.float32
BF16 = jnp.bfloat16
FAR = 1e30
VMEM = pltpu.VMEM
ANY = pl.ANY


def vspec():
    return pl.BlockSpec(memory_space=pltpu.VMEM)


def aspec():
    return pl.BlockSpec(memory_space=pl.ANY)


def sspec():
    return pl.BlockSpec(memory_space=pltpu.SMEM)


def params(collective=None, side=False):
    return pltpu.CompilerParams(
        collective_id=collective, has_side_effects=side, vmem_limit_bytes=60 * 1024 * 1024
    )


def mm_nt(a, b):
    return lax.dot_general(a, b, (((1,), (1,)), ((), ())), preferred_element_type=F32)


def mm_tn(a, b):
    return lax.dot_general(a, b, (((0,), (0,)), ((), ())), preferred_element_type=F32)


def mm(a, b):
    return lax.dot_general(a, b, (((1,), (0,)), ((), ())), preferred_element_type=F32)


def rows(at, count):
    return pl.ds(pl.multiple_of(at, count), count)


def pack_kernel(
    pack_ref, glob_ref, q_ref, do_ref, k_ref, v_ref, table_ref, x_ref, g_ref, out_ref, stats_ref, gp_ref, pp_ref
):
    shards = out_ref.shape[0]
    lane_rows = lax.broadcasted_iota(jnp.int32, (8, 128), 0)

    def one(peer, carry):
        tiles = []
        for slot in range(CAP):
            row = pack_ref[peer * CAP + slot]
            safe = jnp.maximum(row, 0)
            out_ref[peer, slot, 0] = q_ref[rows(safe * BLK, BLK), :]
            out_ref[peer, slot, 1] = do_ref[rows(safe * BLK, BLK), :]
            tiles.append(jnp.where(row >= 0, table_ref[safe], FAR))
        stats_ref[peer] = jnp.where(lane_rows < 4, tiles[0], tiles[1])
        return carry

    lax.fori_loop(0, shards, one, 0)
    for number in range(2):
        place = glob_ref[number]
        safe = jnp.maximum(place, 0)
        for side, ref in enumerate((k_ref, v_ref)):
            piece = ref[rows(safe * BLK, BLK), :].astype(F32)
            gp_ref[pl.ds(side * 2 * BLK + number * BLK, BLK), :] = jnp.where(place >= 0, piece, 0.0)
    pp_ref[...] = mm(x_ref[...], g_ref[...])


def peers_of(axis):
    size = lax.axis_size(axis)
    me = lax.axis_index(axis)
    return size, me


def greet(axes):
    barrier = pltpu.get_barrier_semaphore()
    total = 0
    for axis in axes:
        size, me = peers_of(axis)

        def hello(k, carry, axis=axis, size=size, me=me):
            pl.semaphore_signal(
                barrier, inc=1, device_id={axis: lax.rem(me + k, size)}, device_id_type=MESH
            )
            return carry

        lax.fori_loop(1, size, hello, 0)
        total += size - 1
    pl.semaphore_wait(barrier, total)


def send(axis, peer, src, dst, send_sem, recv_sem):
    pltpu.make_async_remote_copy(
        src_ref=src,
        dst_ref=dst,
        send_sem=send_sem,
        recv_sem=recv_sem,
        device_id={axis: peer},
        device_id_type=MESH,
    ).start()


def order_of(shards):
    wide, tall = shards // 8, 4

    def hops(at):
        return min(at[0], wide - at[0]) + min(at[1], tall - at[1])

    chips = [(2, 2), (2, 1), (2, 3), (1, 2), (3, 2), (2, 0), (0, 2), (1, 1), (3, 3), (1, 3), (3, 1)]
    chips += [(1, 0), (3, 0), (0, 1), (0, 3)]
    if wide != 4:
        chips = [(a, b) for a in range(wide) for b in range(tall) if a or b]
        chips.sort(key=hops, reverse=True)
    return [(a, b, c) for a, b in chips for c in (0, 1)] + [(0, 0, 1)]


def seq_peer(offset, shards, me):
    wide, tall = shards // 8, 4
    x, y, core = me // 8, lax.rem(me // 2, tall), lax.rem(me, 2)
    dx, dy = offset[0], offset[1]
    if wide == tall and dx != dy:
        dx, dy = dx + core * (dy - dx), dy + core * (dx - dy)
    return lax.rem(x + dx, wide) * 8 + lax.rem(y + dy, tall) * 2 + lax.rem(core + offset[2], 2)


def to_all(axis, src_of, dst_of, send_sem, recv_sem):
    size, me = peers_of(axis)
    if axis == "seq":
        for k, offset in enumerate(order_of(size)):
            peer = seq_peer(offset, size, me)
            send(axis, peer, src_of(peer), dst_of(k + 1), send_sem, recv_sem)
        return

    def step(k, carry):
        peer = lax.rem(me + k, size)
        send(axis, peer, src_of(peer), dst_of(k), send_sem, recv_sem)
        return carry

    lax.fori_loop(1, size, step, 0)


def drain(ref, sem):
    pltpu.make_async_copy(ref, ref, sem).wait()


def first_kernel(
    pack_ref, stats_ref, k_ref, v_ref, gp_ref, pp_ref,
    arrived_ref, stats_out, halo_ref, gkv_ref, proj_ref,
    gbuf, gown, gall, pbuf, pown, pall, sems, own_sem,
):
    shards, me = peers_of("seq")
    groups, mz = peers_of("grp")
    tokens = k_ref.shape[0]
    gr = gown.shape[0]
    pr = pown.shape[0]
    greet(("seq", "grp"))
    to_all("seq", lambda p: gp_ref.at[rows(p * gr, gr)], lambda k: gbuf.at[k - 1], sems.at[0], sems.at[1])
    to_all("grp", lambda p: pp_ref.at[rows(p * pr, pr)], lambda k: pbuf.at[k - 1], sems.at[2], sems.at[3])
    nxt, prv = lax.rem(me + 1, shards), lax.rem(me + shards - 1, shards)
    for side, ref in enumerate((k_ref, v_ref)):
        send("seq", nxt, ref.at[pl.ds(tokens - BLK, BLK)], halo_ref.at[0, side], sems.at[4], sems.at[5])
        send("seq", prv, ref.at[pl.ds(0, BLK)], halo_ref.at[1, side], sems.at[4], sems.at[5])
    to_all("seq", lambda p: stats_ref.at[p], lambda k: stats_out.at[me], sems.at[6], sems.at[7])
    to_all("seq", lambda p: pack_ref.at[p], lambda k: arrived_ref.at[me], sems.at[8], sems.at[9])
    own = pltpu.make_async_copy(pack_ref.at[me], arrived_ref.at[me], own_sem.at[0])
    own.start()
    own2 = pltpu.make_async_copy(stats_ref.at[me], stats_out.at[me], own_sem.at[1])
    own2.start()
    drain(gbuf, sems.at[1])
    total = gp_ref[rows(me * gr, gr), :]
    for k in range(shards - 1):
        total = total + gbuf[k]
    gown[...] = total
    gall[rows(me * gr, gr), :] = total
    drain(pbuf, sems.at[3])
    ptotal = pp_ref[rows(mz * pr, pr), :]
    for k in range(groups - 1):
        ptotal = ptotal + pbuf[k]
    pown[...] = ptotal.astype(BF16)
    pall[rows(mz * pr, pr), :] = ptotal.astype(BF16)
    to_all("seq", lambda p: gown, lambda k: gall.at[rows(me * gr, gr)], sems.at[10], sems.at[11])
    to_all("grp", lambda p: pown, lambda k: pall.at[rows(mz * pr, pr)], sems.at[12], sems.at[13])
    drain(pall.at[pl.ds(0, pr * (groups - 1))], sems.at[13])
    proj_ref[...] = pall[...]
    drain(gall.at[pl.ds(0, gr * (shards - 1))], sems.at[11])
    gkv_ref[...] = gall[...]
    own.wait()
    own2.wait()
    drain(halo_ref, sems.at[5])
    drain(stats_out.at[pl.ds(0, shards - 1)], sems.at[7])
    drain(arrived_ref.at[pl.ds(0, shards - 1)], sems.at[9])
    drain(gp_ref.at[pl.ds(0, gr * (shards - 1))], sems.at[0])
    drain(pp_ref.at[pl.ds(0, pr * (groups - 1))], sems.at[2])
    drain(halo_ref, sems.at[4])
    drain(stats_ref.at[pl.ds(0, shards - 1)], sems.at[6])
    drain(pack_ref.at[pl.ds(0, shards - 1)], sems.at[8])
    drain(gall.at[pl.ds(0, gr * (shards - 1))], sems.at[10])
    drain(pall.at[pl.ds(0, pr * (groups - 1))], sems.at[12])


def two_heads(block):
    half = block.shape[1] // 2
    lanes = lax.broadcasted_iota(jnp.int32, block.shape, 1)
    zero = jnp.zeros_like(block)
    return jnp.concatenate(
        [jnp.where(lanes < half, block, zero), jnp.where(lanes >= half, block, zero)], axis=0
    )


def pair(q, do, lse, delta, keys, values, good):
    inverse_root = 1.0 / math.sqrt(q.shape[1] // 2)
    qq, dd = two_heads(q), two_heads(do)
    weights = jnp.exp(mm_nt(keys, qq) * inverse_root - lse)
    if good is not None:
        weights = jnp.where(good, weights, 0.0)
    score = weights * (mm_nt(values, dd) - delta) * inverse_root
    weights_low, score_low = weights.astype(BF16), score.astype(BF16)
    dv = mm(weights_low, dd)
    dk = mm(score_low, qq)
    wide = mm_tn(score_low, keys)
    half = q.shape[1] // 2
    dq = jnp.concatenate([wide[:BLK, :half], wide[BLK:, half:]], axis=1)
    return dq, dk, dv


def attend_kernel(
    serve_ref, meta_ref, q_ref, do_ref, k_ref, v_ref, halo_ref, gkv_ref, table_ref, arr_ref, st_ref,
    ret_ref, dq_ref, acc_ref, gacc_ref, kpad, vpad, gk,
):
    i = pl.program_id(0)
    tokens = k_ref.shape[0]

    @pl.when(i == 0)
    def _():
        for pad, ref, side in ((kpad, k_ref, 0), (vpad, v_ref, 1)):
            pad[pl.ds(0, BLK), :] = halo_ref[0, side]
            pad[pl.ds(BLK, tokens), :] = ref[...]
            pad[pl.ds(BLK + tokens, BLK), :] = halo_ref[1, side]
        gk[...] = gkv_ref[...].astype(BF16)
        acc_ref[...] = jnp.zeros_like(acc_ref)
        gacc_ref[...] = jnp.zeros_like(gacc_ref)

    at = i * BLK
    win = pl.ds(pl.multiple_of(at, BLK), 3 * BLK)
    keys = jnp.concatenate([kpad[win, :], gk[: 2 * BLK, :]], axis=0)
    values = jnp.concatenate([vpad[win, :], gk[2 * BLK :, :]], axis=0)
    row = lax.broadcasted_iota(jnp.int32, (5 * BLK, 2 * BLK), 0)
    low = jnp.where(meta_ref[0] == i, BLK, 0)
    high = jnp.where(meta_ref[1] == i, 2 * BLK, 3 * BLK)
    good = ((row >= low) & (row < high)) | (row >= 3 * BLK)
    stat = table_ref[i]
    dq, dk, dv = pair(
        q_ref[rows(at, BLK), :], do_ref[rows(at, BLK), :], stat[0:1, :], stat[1:2, :], keys, values, good
    )
    dq_ref[...] = dq
    acc_ref[0, win, :] += dk[: 3 * BLK]
    acc_ref[1, win, :] += dv[: 3 * BLK]
    gacc_ref[pl.ds(0, 2 * BLK), :] += dk[3 * BLK :]
    gacc_ref[pl.ds(2 * BLK, 2 * BLK), :] += dv[3 * BLK :]
    per = arr_ref.shape[0]
    for p in range(per):
        for c in range(CAP):
            place = serve_ref[(i * per + p) * CAP + c]
            here = rows((place + 1) * BLK, BLK)
            dq, dk, dv = pair(
                arr_ref[p, c, 0], arr_ref[p, c, 1],
                st_ref[p, 4 * c : 4 * c + 1, :], st_ref[p, 4 * c + 1 : 4 * c + 2, :],
                kpad[here, :], vpad[here, :], None,
            )
            ret_ref[p, c] = dq.astype(BF16)
            acc_ref[0, here, :] += dk
            acc_ref[1, here, :] += dv


def second_kernel(
    ret_ref, acc_ref, gacc_ref, back_ref, hg_ref, gsum_ref, gbuf, gown, gall, sems, own_sem
):
    shards, me = peers_of("seq")
    padded = acc_ref.shape[1]
    gr = gown.shape[0]
    greet(("seq",))
    to_all("seq", lambda p: gacc_ref.at[rows(p * gr, gr)], lambda k: gbuf.at[k - 1], sems.at[0], sems.at[1])
    nxt, prv = lax.rem(me + 1, shards), lax.rem(me + shards - 1, shards)
    for side in range(2):
        send("seq", nxt, acc_ref.at[side, pl.ds(padded - BLK, BLK)], hg_ref.at[0, side], sems.at[2], sems.at[3])
        send("seq", prv, acc_ref.at[side, pl.ds(0, BLK)], hg_ref.at[1, side], sems.at[2], sems.at[3])
    to_all("seq", lambda p: ret_ref.at[p], lambda k: back_ref.at[me], sems.at[4], sems.at[5])
    own = pltpu.make_async_copy(ret_ref.at[me], back_ref.at[me], own_sem)
    own.start()
    drain(gbuf, sems.at[1])
    total = gacc_ref[rows(me * gr, gr), :]
    for k in range(shards - 1):
        total = total + gbuf[k]
    gown[...] = total
    gall[rows(me * gr, gr), :] = total
    to_all("seq", lambda p: gown, lambda k: gall.at[rows(me * gr, gr)], sems.at[6], sems.at[7])
    drain(gall.at[pl.ds(0, gr * (shards - 1))], sems.at[7])
    gsum_ref[...] = gall[...]
    own.wait()
    drain(hg_ref, sems.at[3])
    drain(back_ref.at[pl.ds(0, shards - 1)], sems.at[5])
    drain(gbuf, sems.at[0])
    drain(hg_ref, sems.at[2])
    drain(ret_ref.at[pl.ds(0, shards - 1)], sems.at[4])
    drain(gall.at[pl.ds(0, gr * (shards - 1))], sems.at[6])


def finish_kernel(
    fetch_ref, glob_ref, acc_ref, dq_ref, back_ref, hg_ref, gsum_ref, proj_ref,
    gq_ref, gk_ref, gv_ref, part_ref,
):
    blocks = dq_ref.shape[0] // BLK
    randoms = fetch_ref.shape[0] // blocks
    shards = part_ref.shape[0]
    for b in range(blocks):
        here = pl.ds(b * BLK, BLK)
        total = dq_ref[here, :]
        for j in range(randoms):
            slot = fetch_ref[b * randoms + j]
            total = total + back_ref[slot].astype(F32)
        gq_ref[here, :] = total.astype(BF16)
        for side, out in enumerate((gk_ref, gv_ref)):
            total = acc_ref[side, pl.ds((b + 1) * BLK, BLK), :]
            if b == 0:
                total = total + hg_ref[0, side]
            if b == blocks - 1:
                total = total + hg_ref[1, side]
            for number in range(2):
                piece = gsum_ref[pl.ds(side * 2 * BLK + number * BLK, BLK), :]
                total = total + jnp.where(glob_ref[number] == b, piece, 0.0)
            out[here, :] = total.astype(BF16)
    turned = proj_ref[...].astype(F32).T.astype(BF16)
    width = gq_ref.shape[1]
    for number, ref in enumerate((gq_ref, gk_ref, gv_ref)):
        product = mm(turned, ref[...]).astype(BF16)
        share = product.shape[0] // shards
        part_ref[:, pl.ds(number * share, share), :] = product.reshape(shards, share, width)


def clip_kernel(limit, part_ref, out_ref, fbuf, sq, sbuf, sq2, zbuf, sems):
    shards, me = peers_of("seq")
    groups, mz = peers_of("grp")
    greet(("seq", "grp"))
    to_all("seq", lambda p: part_ref.at[p], lambda k: fbuf.at[k - 1], sems.at[0], sems.at[1])
    drain(fbuf, sems.at[1])
    share = part_ref[me].astype(F32)
    for k in range(shards - 1):
        share = share + fbuf[k].astype(F32)
    own = jnp.sum(share * share, keepdims=True)
    tile = jnp.broadcast_to(own, sq.shape)
    sq[...] = tile
    to_all("seq", lambda p: sq, lambda k: sbuf.at[k - 1], sems.at[2], sems.at[3])
    drain(sbuf, sems.at[3])
    for k in range(shards - 1):
        tile = tile + sbuf[k]
    sq2[...] = tile
    to_all("grp", lambda p: sq2, lambda k: zbuf.at[k - 1], sems.at[4], sems.at[5])
    drain(zbuf, sems.at[5])
    for k in range(groups - 1):
        tile = tile + zbuf[k]
    scale = jnp.minimum(1.0, limit * lax.rsqrt(tile[0:1, 0:1] + 1e-06))
    out_ref[...] = share * scale
    drain(fbuf, sems.at[0])
    drain(sbuf, sems.at[2])
    drain(zbuf, sems.at[4])


def slots(match, payload):
    count = match.shape[-1]
    earlier = (jnp.arange(count)[None, :] < jnp.arange(count)[:, None]).astype(jnp.int32)
    rank = jnp.sum(match[..., None, :] * earlier, axis=-1)
    chosen = match[..., None, :] * (rank[..., None, :] == jnp.arange(CAP)[:, None]).astype(jnp.int32)
    live = jnp.sum(chosen, axis=-1)
    value = jnp.sum(chosen * payload[..., None, :], axis=-1)
    return value, live


def body(
    query_rows, key_rows, value_rows, attn_output, output_grad, row_logsumexp,
    layer_input, galore_proj, rand_owner, rand_local, global_block,
):
    tokens, width = query_rows.shape
    heads = row_logsumexp.shape[0]
    blocks = tokens // BLK
    shards, me = peers_of("seq")
    groups = lax.axis_size("grp")
    randoms = rand_owner.shape[1]
    rank = galore_proj.shape[1]
    asks = blocks * randoms
    all_owner = rand_owner.reshape(shards, asks)
    all_local = rand_local.reshape(shards, asks)
    my_owner = lax.dynamic_slice_in_dim(rand_owner, me * blocks, blocks, 0).reshape(asks)
    ask_match = (my_owner[None, :] == jnp.arange(shards, dtype=jnp.int32)[:, None]).astype(jnp.int32)
    row_of = jnp.broadcast_to((jnp.arange(asks, dtype=jnp.int32) // randoms)[None, :], (shards, asks))
    pack_value, pack_live = slots(ask_match, row_of)
    pack_row = jnp.where(pack_live > 0, pack_value, -1).reshape(-1)
    serve_match = (all_owner == me).astype(jnp.int32)
    serve_block = slots(serve_match, all_local)[0].reshape(-1)
    same = (my_owner[:, None] == my_owner[None, :]).astype(jnp.int32)
    before = (jnp.arange(asks)[None, :] < jnp.arange(asks)[:, None]).astype(jnp.int32)
    fetch = my_owner * CAP + jnp.sum(same * before, axis=1)
    glob_place = jnp.where(global_block // blocks == me, global_block % blocks, -1).astype(jnp.int32)
    edges = jnp.stack(
        [jnp.where(me == 0, 0, -1), jnp.where(me == shards - 1, blocks - 1, -1)]
    ).astype(jnp.int32)
    lse = row_logsumexp.astype(F32).reshape(heads, blocks, BLK).transpose(1, 0, 2).reshape(blocks, heads * BLK)
    delta = jnp.sum(
        (output_grad.astype(F32) * attn_output.astype(F32)).reshape(blocks, BLK, heads, width // heads), axis=3
    )
    delta = delta.transpose(0, 2, 1).reshape(blocks, heads * BLK)
    nil = jnp.zeros_like(lse)
    table = jnp.stack([lse, delta, nil, nil, lse, delta, nil, nil], axis=1)

    pack, stats, glob_piece, proj_piece = pl.pallas_call(
        pack_kernel,
        out_shape=(
            jax.ShapeDtypeStruct((shards, CAP, 2, BLK, width), BF16),
            jax.ShapeDtypeStruct((shards, 8, 128), F32),
            jax.ShapeDtypeStruct((4 * BLK, width), F32),
            jax.ShapeDtypeStruct((tokens, rank), F32),
        ),
        in_specs=[sspec()] * 2 + [vspec()] * 7,
        out_specs=(vspec(),) * 4,
        compiler_params=params(),
        name="pack",
    )(pack_row, glob_place, query_rows, output_grad, key_rows, value_rows, table, layer_input, galore_proj)

    gr = 4 * BLK // shards
    pr = tokens // groups
    arrived, stats_in, halo, glob_kv, projected = pl.pallas_call(
        first_kernel,
        out_shape=(
            jax.ShapeDtypeStruct((shards, CAP, 2, BLK, width), BF16),
            jax.ShapeDtypeStruct((shards, 8, 128), F32),
            jax.ShapeDtypeStruct((2, 2, BLK, width), BF16),
            jax.ShapeDtypeStruct((4 * BLK, width), F32),
            jax.ShapeDtypeStruct((tokens, rank), BF16),
        ),
        in_specs=[aspec(), aspec(), aspec(), aspec(), vspec(), vspec()],
        out_specs=(aspec(), aspec(), aspec(), vspec(), vspec()),
        scratch_shapes=[
            VMEM((shards - 1, gr, width), F32),
            VMEM((gr, width), F32),
            VMEM((4 * BLK, width), F32),
            VMEM((groups - 1, pr, rank), F32),
            VMEM((pr, rank), BF16),
            VMEM((tokens, rank), BF16),
            pltpu.SemaphoreType.DMA((14,)),
            pltpu.SemaphoreType.DMA((2,)),
        ],
        compiler_params=params(1, True),
        name="first_exchange",
    )(pack, stats, key_rows, value_rows, glob_piece, proj_piece)

    per = shards // blocks
    full = lambda *shape: pl.BlockSpec(shape, lambda i, *_: (0,) * len(shape))
    back_out, dq_own, acc, gacc = pl.pallas_call(
        attend_kernel,
        grid_spec=pltpu.PrefetchScalarGridSpec(
            num_scalar_prefetch=2,
            grid=(blocks,),
            in_specs=[
                full(tokens, width),
                full(tokens, width),
                full(tokens, width),
                full(tokens, width),
                full(2, 2, BLK, width),
                full(4 * BLK, width),
                full(blocks, 8, 128),
                pl.BlockSpec((per, CAP, 2, BLK, width), lambda i, *_: (i, 0, 0, 0, 0)),
                pl.BlockSpec((per, 8, 128), lambda i, *_: (i, 0, 0)),
            ],
            out_specs=(
                pl.BlockSpec((per, CAP, BLK, width), lambda i, *_: (i, 0, 0, 0)),
                pl.BlockSpec((BLK, width), lambda i, *_: (i, 0)),
                full(2, tokens + 2 * BLK, width),
                full(4 * BLK, width),
            ),
            scratch_shapes=[
                VMEM((tokens + 2 * BLK, width), BF16),
                VMEM((tokens + 2 * BLK, width), BF16),
                VMEM((4 * BLK, width), BF16),
            ],
        ),
        out_shape=(
            jax.ShapeDtypeStruct((shards, CAP, BLK, width), BF16),
            jax.ShapeDtypeStruct((tokens, width), F32),
            jax.ShapeDtypeStruct((2, tokens + 2 * BLK, width), F32),
            jax.ShapeDtypeStruct((4 * BLK, width), F32),
        ),
        compiler_params=params(),
        name="attend",
    )(
        serve_block, edges, query_rows, output_grad, key_rows, value_rows, halo, glob_kv, table, arrived, stats_in
    )

    back, halo_grad, glob_grad = pl.pallas_call(
        second_kernel,
        out_shape=(
            jax.ShapeDtypeStruct((shards, CAP, BLK, width), BF16),
            jax.ShapeDtypeStruct((2, 2, BLK, width), F32),
            jax.ShapeDtypeStruct((4 * BLK, width), F32),
        ),
        in_specs=[aspec(), aspec(), vspec()],
        out_specs=(aspec(), aspec(), vspec()),
        scratch_shapes=[
            VMEM((shards - 1, gr, width), F32),
            VMEM((gr, width), F32),
            VMEM((4 * BLK, width), F32),
            pltpu.SemaphoreType.DMA((8,)),
            pltpu.SemaphoreType.DMA,
        ],
        compiler_params=params(2, True),
        name="second_exchange",
    )(back_out, acc, gacc)

    share = rank // shards
    grad_query, grad_key, grad_value, part = pl.pallas_call(
        finish_kernel,
        out_shape=(
            jax.ShapeDtypeStruct((tokens, width), BF16),
            jax.ShapeDtypeStruct((tokens, width), BF16),
            jax.ShapeDtypeStruct((tokens, width), BF16),
            jax.ShapeDtypeStruct((shards, 3 * share, width), BF16),
        ),
        in_specs=[sspec()] * 2 + [vspec()] * 6,
        out_specs=(vspec(),) * 4,
        compiler_params=params(),
        name="finish",
    )(fetch, glob_place, acc, dq_own, back.reshape(shards * CAP, BLK, width), halo_grad, glob_grad, projected)

    limit = 0.5 * math.sqrt(3 * rank * width * groups)
    clipped = pl.pallas_call(
        functools.partial(clip_kernel, limit),
        out_shape=jax.ShapeDtypeStruct((3 * share, width), F32),
        in_specs=[vspec()],
        out_specs=vspec(),
        scratch_shapes=[
            VMEM((shards - 1, 3 * share, width), BF16),
            VMEM((8, 128), F32),
            VMEM((shards - 1, 8, 128), F32),
            VMEM((8, 128), F32),
            VMEM((groups - 1, 8, 128), F32),
            pltpu.SemaphoreType.DMA((6,)),
        ],
        compiler_params=params(3, True),
        name="clip",
    )(part)
    return (grad_query, grad_key, grad_value, clipped.reshape(3, share, width))


def solution(mesh):
    in_specs = (
        P("seq", "grp"),
        P("seq", "grp"),
        P("seq", "grp"),
        P("seq", "grp"),
        P("seq", "grp"),
        P("grp", "seq"),
        P("seq", "grp"),
        P("grp", None),
        P(),
        P(),
        P(),
    )
    out_specs = (P("seq", "grp"), P("seq", "grp"), P("seq", "grp"), P(None, "seq", "grp"))
    return jax.shard_map(body, mesh=mesh, in_specs=in_specs, out_specs=out_specs, check_vma=False)
```

```python
import functools
import math

import jax
import jax.numpy as jnp
from jax import lax
from jax.experimental import pallas as pl
from jax.experimental.pallas import tpu as pltpu
from jax.sharding import PartitionSpec as P

BLK = 64
CAP = 2
MESH = pl.DeviceIdType.MESH
F32 = jnp.float32
BF16 = jnp.bfloat16
FAR = 1e30
VMEM = pltpu.VMEM
ANY = pl.ANY


def vspec():
    return pl.BlockSpec(memory_space=pltpu.VMEM)


def aspec():
    return pl.BlockSpec(memory_space=pl.ANY)


def sspec():
    return pl.BlockSpec(memory_space=pltpu.SMEM)


def params(collective=None, side=False):
    return pltpu.CompilerParams(
        collective_id=collective, has_side_effects=side, vmem_limit_bytes=60 * 1024 * 1024
    )


def mm_nt(a, b):
    return lax.dot_general(a, b, (((1,), (1,)), ((), ())), preferred_element_type=F32)


def mm_tn(a, b):
    return lax.dot_general(a, b, (((0,), (0,)), ((), ())), preferred_element_type=F32)


def mm(a, b):
    return lax.dot_general(a, b, (((1,), (0,)), ((), ())), preferred_element_type=F32)


def rows(at, count):
    return pl.ds(pl.multiple_of(at, count), count)


def pack_kernel(
    pack_ref, glob_ref, q_ref, do_ref, k_ref, v_ref, table_ref, x_ref, g_ref, out_ref, stats_ref, gp_ref, pp_ref
):
    shards = out_ref.shape[0]
    lane_rows = lax.broadcasted_iota(jnp.int32, (8, 128), 0)

    def one(peer, carry):
        tiles = []
        for slot in range(CAP):
            row = pack_ref[peer * CAP + slot]
            safe = jnp.maximum(row, 0)
            out_ref[peer, slot, 0] = q_ref[rows(safe * BLK, BLK), :]
            out_ref[peer, slot, 1] = do_ref[rows(safe * BLK, BLK), :]
            tiles.append(jnp.where(row >= 0, table_ref[safe], FAR))
        stats_ref[peer] = jnp.where(lane_rows < 4, tiles[0], tiles[1])
        return carry

    lax.fori_loop(0, shards, one, 0)
    for number in range(2):
        place = glob_ref[number]
        safe = jnp.maximum(place, 0)
        for side, ref in enumerate((k_ref, v_ref)):
            piece = ref[rows(safe * BLK, BLK), :].astype(F32)
            gp_ref[pl.ds(side * 2 * BLK + number * BLK, BLK), :] = jnp.where(place >= 0, piece, 0.0)
    pp_ref[...] = mm(x_ref[...], g_ref[...])


def peers_of(axis):
    size = lax.axis_size(axis)
    me = lax.axis_index(axis)
    return size, me


def greet(axes):
    barrier = pltpu.get_barrier_semaphore()
    total = 0
    for axis in axes:
        size, me = peers_of(axis)

        def hello(k, carry, axis=axis, size=size, me=me):
            pl.semaphore_signal(
                barrier, inc=1, device_id={axis: lax.rem(me + k, size)}, device_id_type=MESH
            )
            return carry

        lax.fori_loop(1, size, hello, 0)
        total += size - 1
    pl.semaphore_wait(barrier, total)


def send(axis, peer, src, dst, send_sem, recv_sem):
    pltpu.make_async_remote_copy(
        src_ref=src,
        dst_ref=dst,
        send_sem=send_sem,
        recv_sem=recv_sem,
        device_id={axis: peer},
        device_id_type=MESH,
    ).start()


def chips_of(shards):
    wide, tall = shards // 8, 4

    def hops(at):
        return min(at[0], wide - at[0]) + min(at[1], tall - at[1])

    chips = [(2, 2), (2, 1), (2, 3), (1, 2), (3, 2), (2, 0), (0, 2), (1, 1), (3, 3), (1, 3), (3, 1)]
    chips += [(1, 0), (3, 0), (0, 1), (0, 3)]
    if wide != 4:
        chips = [(a, b) for a in range(wide) for b in range(tall) if a or b]
        chips.sort(key=hops, reverse=True)
    return [(0, 0)] + chips


def order_of(shards):
    return [(a, b, c) for a, b in chips_of(shards)[1:] for c in (0, 1)] + [(0, 0, 1)]


def seq_peer(offset, shards, me):
    wide, tall = shards // 8, 4
    x, y, core = me // 8, lax.rem(me // 2, tall), lax.rem(me, 2)
    dx, dy = offset[0], offset[1]
    if wide == tall and dx != dy:
        dx, dy = dx + core * (dy - dx), dy + core * (dx - dy)
    return lax.rem(x + dx, wide) * 8 + lax.rem(y + dy, tall) * 2 + lax.rem(core + offset[2], 2)


def to_all(axis, src_of, dst_of, send_sem, recv_sem):
    size, me = peers_of(axis)
    if axis == "seq":
        for k, offset in enumerate(order_of(size)):
            peer = seq_peer(offset, size, me)
            send(axis, peer, src_of(peer), dst_of(k + 1), send_sem, recv_sem)
        return

    def step(k, carry):
        peer = lax.rem(me + k, size)
        send(axis, peer, src_of(peer), dst_of(k), send_sem, recv_sem)
        return carry

    lax.fori_loop(1, size, step, 0)


def drain(ref, sem):
    pltpu.make_async_copy(ref, ref, sem).wait()


def two_heads(block):
    half = block.shape[1] // 2
    lanes = lax.broadcasted_iota(jnp.int32, block.shape, 1)
    zero = jnp.zeros_like(block)
    return jnp.concatenate(
        [jnp.where(lanes < half, block, zero), jnp.where(lanes >= half, block, zero)], axis=0
    )


def pair(q, do, lse, delta, keys, values, good):
    inverse_root = 1.0 / math.sqrt(q.shape[1] // 2)
    qq, dd = two_heads(q), two_heads(do)
    weights = jnp.exp(mm_nt(keys, qq) * inverse_root - lse)
    if good is not None:
        weights = jnp.where(good, weights, 0.0)
    score = weights * (mm_nt(values, dd) - delta) * inverse_root
    weights_low, score_low = weights.astype(BF16), score.astype(BF16)
    dv = mm(weights_low, dd)
    dk = mm(score_low, qq)
    wide = mm_tn(score_low, keys)
    half = q.shape[1] // 2
    dq = jnp.concatenate([wide[:BLK, :half], wide[BLK:, half:]], axis=1)
    return dq, dk, dv


def pick(k, values):
    found = values[0]
    for at, value in enumerate(values[1:], 1):
        found = jnp.where(k == at, value, found)
    return found


def main_kernel(
    serve_ref, fetch_ref, pack_ref, stats_ref, q_ref, do_ref, k_ref, v_ref, table_ref, gp_ref, pp_ref,
    gq_ref, own_ref, sg_ref, gsum_ref, proj_ref,
    kpad, vpad, acc, dq, gk, gacc, arrived, stats_in, ret, back, halo, hg,
    gbuf, gown, gall, g2buf, g2own, g2all, pbuf, pown, pall, sems, rsem, own_sem,
):
    shards, me = peers_of("seq")
    groups, mz = peers_of("grp")
    tokens = k_ref.shape[0]
    blocks = tokens // BLK
    randoms = fetch_ref.shape[0] // blocks
    gr = gown.shape[0]
    pr = pown.shape[0]
    chips = chips_of(shards)
    near = len(chips) // 3
    wide, tall = shards // 8, 4
    x, y, core = me // 8, lax.rem(me // 2, tall), lax.rem(me, 2)

    def source(k, dc):
        dx, dy = pick(k, [a for a, _ in chips]), pick(k, [b for _, b in chips])
        theirs = lax.rem(core + dc, 2)
        if wide == tall:
            dx, dy = dx + theirs * (dy - dx), dy + theirs * (dx - dy)
        return lax.rem(x - dx + wide, wide) * 8 + lax.rem(y - dy + tall, tall) * 2 + theirs

    def bulk(first, last):
        for k in range(first, last):
            for dc in range(2):
                if k == 0 and dc == 0:
                    continue
                peer = seq_peer(chips[k] + (dc,), shards, me)
                send("seq", peer, pack_ref.at[peer], arrived.at[me], sems.at[8], rsem.at[2 * k + dc])

    greet(("seq", "grp"))
    to_all("seq", lambda p: gp_ref.at[rows(p * gr, gr)], lambda k: gbuf.at[k - 1], sems.at[0], sems.at[1])
    nxt, prv = lax.rem(me + 1, shards), lax.rem(me + shards - 1, shards)
    for side, ref in enumerate((k_ref, v_ref)):
        send("seq", nxt, ref.at[pl.ds(tokens - BLK, BLK)], halo.at[0, side], sems.at[4], sems.at[5])
        send("seq", prv, ref.at[pl.ds(0, BLK)], halo.at[1, side], sems.at[4], sems.at[5])
    to_all("seq", lambda p: stats_ref.at[p], lambda k: stats_in.at[me], sems.at[6], sems.at[7])
    pltpu.make_async_copy(stats_ref.at[me], stats_in.at[me], own_sem.at[0]).start()
    pltpu.make_async_copy(pack_ref.at[me], arrived.at[me], rsem.at[0]).start()
    bulk(0, near)
    to_all("grp", lambda p: pp_ref.at[rows(p * pr, pr)], lambda k: pbuf.at[k - 1], sems.at[2], sems.at[3])
    drain(gbuf, sems.at[1])
    total = gp_ref[rows(me * gr, gr), :]
    for k in range(shards - 1):
        total = total + gbuf[k]
    gown[...] = total
    gall[rows(me * gr, gr), :] = total
    acc[...] = jnp.zeros_like(acc)
    gacc[...] = jnp.zeros_like(gacc)
    for pad, ref in ((kpad, k_ref), (vpad, v_ref)):
        pad[pl.ds(1, blocks)] = ref[...].reshape(blocks, BLK, ref.shape[1])
    to_all("seq", lambda p: gown, lambda k: gall.at[rows(me * gr, gr)], sems.at[10], sems.at[11])
    bulk(near, len(chips))
    drain(halo, sems.at[5])
    for side, pad in enumerate((kpad, vpad)):
        pad[0] = halo[0, side]
        pad[blocks + 1] = halo[1, side]

    def window(i, carry):
        at = rows(i * BLK, BLK)
        win = pl.ds(pl.multiple_of(i * BLK, BLK), 3 * BLK)
        row = lax.broadcasted_iota(jnp.int32, (3 * BLK, 2 * BLK), 0)
        low = jnp.where((me == 0) & (i == 0), BLK, 0)
        high = jnp.where((me == shards - 1) & (i == blocks - 1), 2 * BLK, 3 * BLK)
        stat = table_ref[i]
        piece, dk, dv = pair(
            q_ref[at, :], do_ref[at, :], stat[0:1, :], stat[1:2, :], kpad[pl.ds(i, 3)].reshape(3 * BLK, -1),
            vpad[pl.ds(i, 3)].reshape(3 * BLK, -1),
            (row >= low) & (row < high),
        )
        dq[at, :] = piece
        acc[0, win, :] += dk
        acc[1, win, :] += dv
        return carry

    lax.fori_loop(0, blocks, window, 0)
    drain(pbuf, sems.at[3])
    ptotal = pp_ref[rows(mz * pr, pr), :]
    for k in range(groups - 1):
        ptotal = ptotal + pbuf[k]
    pown[...] = ptotal.astype(BF16)
    pall[rows(mz * pr, pr), :] = ptotal.astype(BF16)
    for side in range(2):
        send("seq", nxt, acc.at[side, pl.ds(BLK + tokens, BLK)], hg.at[0, side], sems.at[14], sems.at[15])
        send("seq", prv, acc.at[side, pl.ds(0, BLK)], hg.at[1, side], sems.at[14], sems.at[15])
    drain(stats_in.at[pl.ds(0, shards - 1)], sems.at[7])
    pltpu.make_async_copy(stats_ref.at[me], stats_in.at[me], own_sem.at[0]).wait()

    def answer(k, dc):
        home = source(k, dc)
        send("seq", home, ret.at[home], back.at[pl.ds(me * CAP, CAP)], sems.at[16], sems.at[17])

    def slot_step(k, carry):
        for dc in range(2):
            home = source(k, dc)
            drain(arrived.at[home], rsem.at[2 * k + dc])
        for dc in range(2):
            home = source(k, dc)
            for c in range(CAP):
                place = serve_ref[home * CAP + c]
                piece, dk, dv = pair(
                    arrived[home, c, 0], arrived[home, c, 1],
                    stats_in[home, 4 * c : 4 * c + 1, :], stats_in[home, 4 * c + 1 : 4 * c + 2, :],
                    kpad[place], vpad[place], None,
                )
                ret[home, c] = piece.astype(BF16)
                sg_ref[home * CAP + c, 0] = dk.astype(BF16)
                sg_ref[home * CAP + c, 1] = dv.astype(BF16)

        @pl.when(k >= 2)
        def _():
            for dc in range(2):
                answer(k - 1, dc)

        return carry

    def globals_step(i, carry):
        at = rows(i * BLK, BLK)
        stat = table_ref[i]
        piece, dk, dv = pair(
            q_ref[at, :], do_ref[at, :], stat[0:1, :], stat[1:2, :], gk[: 2 * BLK, :], gk[2 * BLK :, :], None
        )
        dq[at, :] += piece
        gacc[pl.ds(0, 2 * BLK), :] += dk
        gacc[pl.ds(2 * BLK, 2 * BLK), :] += dv
        return carry

    count = len(chips)
    lax.fori_loop(0, near, slot_step, 0)
    to_all("grp", lambda p: pown, lambda k: pall.at[rows(mz * pr, pr)], sems.at[12], sems.at[13])
    drain(gall.at[pl.ds(0, gr * (shards - 1))], sems.at[11])
    gk[...] = gall[...].astype(BF16)
    lax.fori_loop(0, blocks, globals_step, 0)
    lax.fori_loop(near, near + 2, slot_step, 0)
    to_all("seq", lambda p: gacc.at[rows(p * gr, gr)], lambda k: g2buf.at[k - 1], sems.at[18], sems.at[19])
    lax.fori_loop(near + 2, count - 2, slot_step, 0)
    drain(g2buf, sems.at[19])
    total = gacc[rows(me * gr, gr), :]
    for k in range(shards - 1):
        total = total + g2buf[k]
    g2own[...] = total
    g2all[rows(me * gr, gr), :] = total
    lax.fori_loop(count - 2, count, slot_step, 0)
    to_all("seq", lambda p: g2own, lambda k: g2all.at[rows(me * gr, gr)], sems.at[20], sems.at[21])
    for dc in range(2):
        answer(count - 1, dc)
    answer(0, 1)
    mine = pltpu.make_async_copy(ret.at[me], back.at[pl.ds(me * CAP, CAP)], own_sem.at[1])
    mine.start()
    drain(hg, sems.at[15])
    for side in range(2):
        own_ref[side] = acc[side, pl.ds(BLK, tokens), :]
        own_ref[side, pl.ds(0, BLK), :] += hg[0, side]
        own_ref[side, pl.ds(tokens - BLK, BLK), :] += hg[1, side]
    drain(pall.at[pl.ds(0, pr * (groups - 1))], sems.at[13])
    proj_ref[...] = pall[...]
    drain(g2all.at[pl.ds(0, gr * (shards - 1))], sems.at[21])
    gsum_ref[...] = g2all[...]
    mine.wait()
    drain(back.at[pl.ds(0, CAP * (shards - 1))], sems.at[17])
    for b in range(blocks):
        total = dq[pl.ds(b * BLK, BLK), :]
        for j in range(randoms):
            total = total + back[fetch_ref[b * randoms + j]].astype(F32)
        gq_ref[pl.ds(b * BLK, BLK), :] = total.astype(BF16)
    drain(gbuf, sems.at[0])
    drain(pbuf, sems.at[2])
    drain(halo, sems.at[4])
    drain(stats_in.at[pl.ds(0, shards - 1)], sems.at[6])
    drain(arrived.at[pl.ds(0, shards - 1)], sems.at[8])
    drain(gall.at[pl.ds(0, gr * (shards - 1))], sems.at[10])
    drain(pall.at[pl.ds(0, pr * (groups - 1))], sems.at[12])
    drain(hg, sems.at[14])
    drain(back.at[pl.ds(0, CAP * (shards - 1))], sems.at[16])
    drain(g2buf, sems.at[18])
    drain(g2all.at[pl.ds(0, gr * (shards - 1))], sems.at[20])


def finish_kernel(serve_ref, glob_ref, own_ref, sg_ref, gsum_ref, proj_ref, gq_ref, gk_ref, gv_ref, part_ref, acc):
    blocks = gq_ref.shape[0] // BLK
    shards = part_ref.shape[0]
    acc[...] = own_ref[...]

    def add(s, carry):
        here = rows((serve_ref[s] - 1) * BLK, BLK)
        for side in range(2):
            acc[side, here, :] += sg_ref[s, side].astype(F32)
        return carry

    lax.fori_loop(0, shards * CAP, add, 0)
    for number in range(2):
        place = glob_ref[number]
        here = rows(jnp.maximum(place, 0) * BLK, BLK)
        for side in range(2):
            piece = gsum_ref[pl.ds(side * 2 * BLK + number * BLK, BLK), :]
            acc[side, here, :] += jnp.where(place >= 0, piece, 0.0)
    for side, out in enumerate((gk_ref, gv_ref)):
        out[...] = acc[side].astype(BF16)
    turned = proj_ref[...].astype(F32).T.astype(BF16)
    width = gq_ref.shape[1]
    for number, ref in enumerate((gq_ref, gk_ref, gv_ref)):
        product = mm(turned, ref[...]).astype(BF16)
        share = product.shape[0] // shards
        part_ref[:, pl.ds(number * share, share), :] = product.reshape(shards, share, width)


def clip_kernel(limit, part_ref, out_ref, fbuf, sq, sbuf, sq2, zbuf, sems):
    shards, me = peers_of("seq")
    groups, mz = peers_of("grp")
    greet(("seq", "grp"))
    to_all("seq", lambda p: part_ref.at[p], lambda k: fbuf.at[k - 1], sems.at[0], sems.at[1])
    drain(fbuf, sems.at[1])
    share = part_ref[me].astype(F32)
    for k in range(shards - 1):
        share = share + fbuf[k].astype(F32)
    own = jnp.sum(share * share, keepdims=True)
    tile = jnp.broadcast_to(own, sq.shape)
    sq[...] = tile
    to_all("seq", lambda p: sq, lambda k: sbuf.at[k - 1], sems.at[2], sems.at[3])
    drain(sbuf, sems.at[3])
    for k in range(shards - 1):
        tile = tile + sbuf[k]
    sq2[...] = tile
    to_all("grp", lambda p: sq2, lambda k: zbuf.at[k - 1], sems.at[4], sems.at[5])
    drain(zbuf, sems.at[5])
    for k in range(groups - 1):
        tile = tile + zbuf[k]
    scale = jnp.minimum(1.0, limit * lax.rsqrt(tile[0:1, 0:1] + 1e-06))
    out_ref[...] = share * scale
    drain(fbuf, sems.at[0])
    drain(sbuf, sems.at[2])
    drain(zbuf, sems.at[4])


def slots(match, payload):
    count = match.shape[-1]
    earlier = (jnp.arange(count)[None, :] < jnp.arange(count)[:, None]).astype(jnp.int32)
    rank = jnp.sum(match[..., None, :] * earlier, axis=-1)
    chosen = match[..., None, :] * (rank[..., None, :] == jnp.arange(CAP)[:, None]).astype(jnp.int32)
    live = jnp.sum(chosen, axis=-1)
    value = jnp.sum(chosen * payload[..., None, :], axis=-1)
    return value, live


def body(
    query_rows, key_rows, value_rows, attn_output, output_grad, row_logsumexp,
    layer_input, galore_proj, rand_owner, rand_local, global_block,
):
    tokens, width = query_rows.shape
    heads = row_logsumexp.shape[0]
    blocks = tokens // BLK
    shards, me = peers_of("seq")
    groups = lax.axis_size("grp")
    randoms = rand_owner.shape[1]
    rank = galore_proj.shape[1]
    asks = blocks * randoms
    all_owner = rand_owner.reshape(shards, asks)
    all_local = rand_local.reshape(shards, asks)
    my_owner = lax.dynamic_slice_in_dim(rand_owner, me * blocks, blocks, 0).reshape(asks)
    ask_match = (my_owner[None, :] == jnp.arange(shards, dtype=jnp.int32)[:, None]).astype(jnp.int32)
    row_of = jnp.broadcast_to((jnp.arange(asks, dtype=jnp.int32) // randoms)[None, :], (shards, asks))
    pack_value, pack_live = slots(ask_match, row_of)
    pack_row = jnp.where(pack_live > 0, pack_value, -1).reshape(-1)
    serve_match = (all_owner == me).astype(jnp.int32)
    serve_block = slots(serve_match, all_local)[0].reshape(-1) + 1
    same = (my_owner[:, None] == my_owner[None, :]).astype(jnp.int32)
    before = (jnp.arange(asks)[None, :] < jnp.arange(asks)[:, None]).astype(jnp.int32)
    fetch = my_owner * CAP + jnp.sum(same * before, axis=1)
    glob_place = jnp.where(global_block // blocks == me, global_block % blocks, -1).astype(jnp.int32)
    lse = row_logsumexp.astype(F32).reshape(heads, blocks, BLK).transpose(1, 0, 2).reshape(blocks, heads * BLK)
    delta = jnp.sum(
        (output_grad.astype(F32) * attn_output.astype(F32)).reshape(blocks, BLK, heads, width // heads), axis=3
    )
    delta = delta.transpose(0, 2, 1).reshape(blocks, heads * BLK)
    nil = jnp.zeros_like(lse)
    table = jnp.stack([lse, delta, nil, nil, lse, delta, nil, nil], axis=1)

    pack, stats, glob_piece, proj_piece = pl.pallas_call(
        pack_kernel,
        out_shape=(
            jax.ShapeDtypeStruct((shards, CAP, 2, BLK, width), BF16),
            jax.ShapeDtypeStruct((shards, 8, 128), F32),
            jax.ShapeDtypeStruct((4 * BLK, width), F32),
            jax.ShapeDtypeStruct((tokens, rank), F32),
        ),
        in_specs=[sspec()] * 2 + [vspec()] * 7,
        out_specs=(vspec(),) * 4,
        compiler_params=params(),
        name="pack",
    )(pack_row, glob_place, query_rows, output_grad, key_rows, value_rows, table, layer_input, galore_proj)

    gr = 4 * BLK // shards
    pr = tokens // groups
    share = rank // shards
    grad_query, own, slot_grads, glob_grad, projected = pl.pallas_call(
        main_kernel,
        out_shape=(
            jax.ShapeDtypeStruct((tokens, width), BF16),
            jax.ShapeDtypeStruct((2, tokens, width), F32),
            jax.ShapeDtypeStruct((shards * CAP, 2, BLK, width), BF16),
            jax.ShapeDtypeStruct((4 * BLK, width), F32),
            jax.ShapeDtypeStruct((tokens, rank), BF16),
        ),
        in_specs=[sspec()] * 2 + [aspec()] * 2 + [vspec()] * 7,
        out_specs=(vspec(),) * 5,
        scratch_shapes=[
            VMEM((blocks + 2, BLK, width), BF16),
            VMEM((blocks + 2, BLK, width), BF16),
            VMEM((2, tokens + 2 * BLK, width), F32),
            VMEM((tokens, width), F32),
            VMEM((4 * BLK, width), BF16),
            VMEM((4 * BLK, width), F32),
            VMEM((shards, CAP, 2, BLK, width), BF16),
            VMEM((shards, 8, 128), F32),
            VMEM((shards, CAP, BLK, width), BF16),
            VMEM((shards * CAP, BLK, width), BF16),
            VMEM((2, 2, BLK, width), BF16),
            VMEM((2, 2, BLK, width), F32),
            VMEM((shards - 1, gr, width), F32),
            VMEM((gr, width), F32),
            VMEM((4 * BLK, width), F32),
            VMEM((shards - 1, gr, width), F32),
            VMEM((gr, width), F32),
            VMEM((4 * BLK, width), F32),
            VMEM((groups - 1, pr, rank), F32),
            VMEM((pr, rank), BF16),
            VMEM((tokens, rank), BF16),
            pltpu.SemaphoreType.DMA((22,)),
            pltpu.SemaphoreType.DMA((shards,)),
            pltpu.SemaphoreType.DMA((2,)),
        ],
        compiler_params=params(1, True),
        name="exchange_attend",
    )(
        serve_block, fetch, pack, stats, query_rows, output_grad, key_rows, value_rows, table, glob_piece, proj_piece
    )

    grad_key, grad_value, part = pl.pallas_call(
        finish_kernel,
        out_shape=(
            jax.ShapeDtypeStruct((tokens, width), BF16),
            jax.ShapeDtypeStruct((tokens, width), BF16),
            jax.ShapeDtypeStruct((shards, 3 * share, width), BF16),
        ),
        in_specs=[sspec()] * 2 + [vspec()] * 5,
        out_specs=(vspec(),) * 3,
        scratch_shapes=[VMEM((2, tokens, width), F32)],
        compiler_params=params(),
        name="finish",
    )(serve_block, glob_place, own, slot_grads, glob_grad, projected, grad_query)

    limit = 0.5 * math.sqrt(3 * rank * width * groups)
    clipped = pl.pallas_call(
        functools.partial(clip_kernel, limit),
        out_shape=jax.ShapeDtypeStruct((3 * share, width), F32),
        in_specs=[vspec()],
        out_specs=vspec(),
        scratch_shapes=[
            VMEM((shards - 1, 3 * share, width), BF16),
            VMEM((8, 128), F32),
            VMEM((shards - 1, 8, 128), F32),
            VMEM((8, 128), F32),
            VMEM((groups - 1, 8, 128), F32),
            pltpu.SemaphoreType.DMA((6,)),
        ],
        compiler_params=params(3, True),
        name="clip",
    )(part)
    return (grad_query, grad_key, grad_value, clipped.reshape(3, share, width))


def solution(mesh):
    in_specs = (
        P("seq", "grp"),
        P("seq", "grp"),
        P("seq", "grp"),
        P("seq", "grp"),
        P("seq", "grp"),
        P("grp", "seq"),
        P("seq", "grp"),
        P("grp", None),
        P(),
        P(),
        P(),
    )
    out_specs = (P("seq", "grp"), P("seq", "grp"), P("seq", "grp"), P(None, "seq", "grp"))
    return jax.shard_map(body, mesh=mesh, in_specs=in_specs, out_specs=out_specs, check_vma=False)
```
